128 devices in a mesh: dp: 8 (over z_lo, y), tensor: 16 (over z_hi, x, core).
Axes of the slice: x: 4, y: 4, z: 4 (z_hi: 2, z_lo: 2; z = z_hi * 2 + z_lo), core: 2. Of those that a mesh axis runs over, the one named last changes fastest.
Arguments:
- block_input: bfloat16 [16384, 1024], P(('dp', 'tensor')), may hold values from -6 to 6
- segment_ids: int32 [16, 1024], P('dp'), may hold values from 0 to 3, never falling along the last dimension, each value on 1 to 512 neighbouring positions
- qkv_weight: bfloat16 [3, 1024, 1024], P(None, None, 'tensor'), may hold values from -1 to 1
- qv_bias: float32 [2, 1024], P(None, 'tensor'), may hold values from -3 to 3
- out_weight: bfloat16 [1024, 1024], P('tensor'), may hold values from -1.5 to 1.5
- out_bias: float32 [1024], replicated, may hold values from -3 to 3
- norm1_gain: float32 [1024], replicated, may hold values from 0.5 to 1.5
- norm1_bias: float32 [1024], replicated, may hold values from -3 to 3
- up_weight: bfloat16 [1024, 4096], P(None, 'tensor'), may hold values from -0.1875 to 0.1875
- up_bias: float32 [4096], P('tensor'), may hold values from -3 to 3
- down_weight: bfloat16 [4096, 1024], P('tensor'), may hold values from -0.09375 to 0.09375
- down_bias: float32 [1024], replicated, may hold values from -3 to 3
- norm2_gain: float32 [1024], replicated, may hold values from 0.5 to 1.5
- norm2_bias: float32 [1024], replicated, may hold values from -3 to 3
- cotangent: bfloat16 [16384, 1024], P(('dp', 'tensor')), may hold values from -6 to 6
Outputs:
- layer_output: bfloat16 [16384, 1024], P(('dp', 'tensor'))
- input_grad: bfloat16 [16384, 1024], P(('dp', 'tensor'))
- grad_qkv: float32 [3, 1024, 1024], P(None, None, 'tensor')
- grad_qv_bias: float32 [2, 1024], P(None, 'tensor')
- grad_out_proj: float32 [1024, 1024], P('tensor')
- grad_out_bias: float32 [1024], replicated
- grad_gain_one: float32 [1024], replicated
- grad_bias_one: float32 [1024], replicated
- grad_up: float32 [1024, 4096], P(None, 'tensor')
- grad_up_bias: float32 [4096], P('tensor')
- grad_down: float32 [4096, 1024], P('tensor')
- grad_down_bias: float32 [1024], replicated
- grad_gain_two: float32 [1024], replicated
- grad_bias_two: float32 [1024], replicated
The draws below stay inside these ranges and needn't reach their ends.
Inputs may be any that keep to these rules, and one draw needn't show every extreme that they name: `segment_ids`: document numbers never fall along a sequence; each document holds 1 to 512 tokens.
All inputs are finite; a program needn't handle non-finite values.
Results may differ from the reference program's by a relative error of at most 0.023.
The reference program's roundings to bfloat16 on the way count: a program that leaves them out, or rounds other values in their place, can miss the bound.
Values may be sent and summed in bfloat16 or wider, within the bound.
A program may use at most 128 MiB of HBM per device.

```python
import math
import jax
import jax.numpy as jnp
import numpy as np
from jax import lax

D = 1024
HEADS = 16
HEAD_DIM = 64
FF = 4096
SEQ = 1024
DOCS = 4
DOC_MOST = 512
SEQS = 16
TOKENS = 16384


def draw_block_input(key, part):
    return jax.random.truncated_normal(key, -6.0, 6.0, (TOKENS, D), jnp.float32).astype(jnp.bfloat16)


def draw_qkv_weight(key, part):
    base = jax.random.truncated_normal(key, -5.0, 5.0, (3, D, D), jnp.float32) * D ** (-0.5)
    return jnp.clip(base, -1.0, 1.0).astype(jnp.bfloat16)


def block_scale(rng, dims, pieces, smallest, high):
    level = 1.0
    for axis_at, parts in pieces:
        draws = jax.random.uniform(jax.random.fold_in(jax.random.fold_in(rng, 6), axis_at), (parts,), jnp.float32, smallest / len(pieces), high / len(pieces))
        level = level * jnp.repeat(jnp.exp(draws), dims[axis_at] // parts).reshape((-1,) + (1,) * (len(dims) - 1 - axis_at))
    return level


def length_profile(amount, total, reach, skew):
    loads = [(1 << 20) // math.isqrt(grade ** skew) + 1 for grade in range(2, amount + 1)]
    surplus, counts = total - reach - (amount - 1), [1] * (amount - 1)
    while surplus > 0:
        candidates = [i for i in range(amount - 1) if counts[i] < reach]
        mass, budget = sum([loads[i] for i in candidates]), surplus
        for i in candidates:
            addition = min(reach - counts[i], max(1, budget * loads[i] // mass), surplus)
            counts[i] = counts[i] + addition
            surplus = surplus - addition
    return np.array([reach] + counts)


def ragged(key, count, total, limit, lean):
    if count == 2:
        one = jax.random.randint(key, (), max(1, total - limit), min(limit, total - 1) + 1)
        return jnp.stack([one, total - one])
    tallies = jnp.asarray(length_profile(count, total, limit, lean), jnp.int32)
    pairs = (count - 1) // 2
    donor, sink = tallies[1:1 + 2 * pairs:2], tallies[2:2 + 2 * pairs:2]
    slack = jnp.minimum(donor - 1, limit - sink)
    moved = jax.random.randint(jax.random.fold_in(key, 1), (pairs,), 0, 1 << 20) % (slack + 1)
    tallies = tallies.at[1:1 + 2 * pairs:2].set(donor - moved).at[2:2 + 2 * pairs:2].set(sink + moved)
    return tallies[jax.random.permutation(jax.random.fold_in(key, 2), count)]


def bell_draw(own_key, shape, scale, reach, cuts=(), kind=jnp.bfloat16):
    loudness = block_scale(own_key, shape, cuts, -0.22, 0.18) if cuts else 1.0
    result = jax.random.normal(own_key, shape, jnp.float32) * scale * loudness
    return jnp.minimum(jnp.maximum(result, -reach), reach).astype(kind)


def setup_inputs(seed: int = 0) -> dict:
    arg_keys = jax.random.split(jax.random.key(seed), 16)
    block_input = draw_block_input(jax.random.fold_in(arg_keys[15], 71), 0)
    segment_ids = jax.vmap(lambda own: jnp.searchsorted(jnp.cumsum(ragged(own, DOCS, SEQ, DOC_MOST, 1)), jnp.arange(SEQ), side="right"))(jax.random.split(arg_keys[1], SEQS)).reshape((SEQS, SEQ)).astype(jnp.int32)
    qkv_weight = draw_qkv_weight(jax.random.fold_in(arg_keys[15], 71), 0)
    qv_bias = bell_draw(arg_keys[3], (2, D), 0.5, 3.0, ((1, 16),), jnp.float32)
    out_weight = bell_draw(arg_keys[4], (D, D), (D // 64) ** -0.5, 1.5, ((0, 16),))
    out_bias = bell_draw(arg_keys[5], (D,), 0.5, 3.0, (), jnp.float32)
    norm1_gain = jnp.clip(1.0 + 0.1 * jax.random.normal(arg_keys[6], (D,), jnp.float32), 0.5, 1.5)
    norm1_bias = bell_draw(arg_keys[7], (D,), 0.5, 3.0, (), jnp.float32)
    up_weight = bell_draw(arg_keys[8], (D, FF), D ** -0.5, 0.1875, ((1, 16),))
    up_bias = bell_draw(arg_keys[9], (FF,), 0.5, 3.0, ((0, 16),), jnp.float32)
    down_weight = bell_draw(arg_keys[10], (FF, D), FF ** -0.5, 0.09375, ((0, 16),))
    down_bias = bell_draw(arg_keys[11], (D,), 0.5, 3.0, (), jnp.float32)
    norm2_gain = jnp.clip(1.0 + 0.1 * jax.random.normal(arg_keys[12], (D,), jnp.float32), 0.5, 1.5)
    norm2_bias = bell_draw(arg_keys[13], (D,), 0.5, 3.0, (), jnp.float32)
    cotangent = bell_draw(arg_keys[14], (TOKENS, D), 1.0, 6.0, ((0, 128),))
    return {"block_input": block_input, "segment_ids": segment_ids, "qkv_weight": qkv_weight, "qv_bias": qv_bias, "out_weight": out_weight, "out_bias": out_bias, "norm1_gain": norm1_gain, "norm1_bias": norm1_bias, "up_weight": up_weight, "up_bias": up_bias, "down_weight": down_weight, "down_bias": down_bias, "norm2_gain": norm2_gain, "norm2_bias": norm2_bias, "cotangent": cotangent}


EPS = 1e-12
MASKED = -1e+30
ROOT_HALF = 0.7071067811865476
INV_ROOT_TAU = 0.3989422804014327

def layer_norm(rows, gain, shift):
    center = rows - lax.optimization_barrier(jnp.mean(rows, axis=-1, keepdims=True))
    inverse = lax.rsqrt(lax.optimization_barrier(jnp.mean(center * center, axis=-1, keepdims=True)) + EPS)
    normed = center * inverse
    return (normed * gain + shift, normed, inverse)

def norm_back(grad, normed, inverse, gain):
    scaled = grad * gain
    return inverse * (scaled - lax.optimization_barrier(jnp.mean(scaled, axis=-1, keepdims=True)) - normed * lax.optimization_barrier(jnp.mean(scaled * normed, axis=-1, keepdims=True)))

def gelu_parts(pre):
    cumul = 0.5 * (1.0 + lax.erf(pre * ROOT_HALF))
    return (pre * cumul, cumul + pre * jnp.exp(-0.5 * pre * pre) * INV_ROOT_TAU)

def masked_scores(queries, keys, segs):
    scores = jnp.einsum('qhd,khd->hqk', queries.astype(jnp.float32), keys.astype(jnp.float32)) * HEAD_DIM ** (-0.5)
    allowed = segs[:, None] == segs[None, :]
    return jnp.where(allowed[None], scores, MASKED)

def attend(queries, keys, values, segs):
    masked = masked_scores(queries, keys, segs)
    top = lax.optimization_barrier(jnp.max(masked, axis=-1, keepdims=True))
    lse = top + jnp.log(lax.optimization_barrier(jnp.sum(jnp.exp(masked - top), axis=-1, keepdims=True)))
    probs = jnp.exp(masked - lse).astype(jnp.bfloat16)
    context = jnp.einsum('hqk,khd->qhd', probs.astype(jnp.float32), values.astype(jnp.float32))
    return (context.astype(jnp.bfloat16), lse)

def attend_back(queries, keys, values, segs, lse, d_context):
    masked = masked_scores(queries, keys, segs)
    probs = jnp.exp(masked - lse)
    probs_half = probs.astype(jnp.bfloat16)
    d_values = jnp.einsum('hqk,qhd->khd', probs_half.astype(jnp.float32), d_context.astype(jnp.float32))
    d_probs = jnp.einsum('qhd,khd->hqk', d_context.astype(jnp.float32), values.astype(jnp.float32))
    d_scores = probs * (d_probs - lax.optimization_barrier(jnp.sum(probs * d_probs, axis=-1, keepdims=True))) * HEAD_DIM ** (-0.5)
    d_scores = d_scores.astype(jnp.bfloat16).astype(jnp.float32)
    d_queries = jnp.einsum('hqk,khd->qhd', d_scores, keys.astype(jnp.float32))
    d_keys = jnp.einsum('hqk,qhd->khd', d_scores, queries.astype(jnp.float32))
    return (d_queries, d_keys, d_values)

def split_heads(arr):
    return arr.reshape(SEQ, HEADS, HEAD_DIM)

def reference(block_input, segment_ids, qkv_weight, qv_bias, out_weight, out_bias, norm1_gain, norm1_bias, up_weight, up_bias, down_weight, down_bias, norm2_gain, norm2_bias, cotangent):
    inputs = block_input.reshape(SEQS, SEQ, D)
    cots = cotangent.reshape(SEQS, SEQ, D)

    def one_sequence(totals, items):
        rows, segs, cot = items
        proj = [jnp.dot(rows, qkv_weight[slot], preferred_element_type=jnp.float32) for slot in range(3)]
        queries = (proj[0] + qv_bias[0]).astype(jnp.bfloat16)
        keys = proj[1].astype(jnp.bfloat16)
        values = (proj[2] + qv_bias[1]).astype(jnp.bfloat16)
        context, lse = attend(split_heads(queries), split_heads(keys), split_heads(values), segs)
        context = context.reshape(SEQ, D)
        first = rows.astype(jnp.float32) + jnp.dot(context, out_weight, preferred_element_type=jnp.float32) + out_bias
        hidden, normed_one, inverse_one = layer_norm(first, norm1_gain, norm1_bias)
        hidden_half = hidden.astype(jnp.bfloat16)
        pre = jnp.dot(hidden_half, up_weight, preferred_element_type=jnp.float32) + up_bias
        act, slope = gelu_parts(pre)
        act_half = act.astype(jnp.bfloat16)
        second = hidden + jnp.dot(act_half, down_weight, preferred_element_type=jnp.float32) + down_bias
        output, normed_two, inverse_two = layer_norm(second, norm2_gain, norm2_bias)
        grad = cot.astype(jnp.float32)
        g_gain_two = lax.optimization_barrier(jnp.sum(grad * normed_two, axis=0))
        g_bias_two = lax.optimization_barrier(jnp.sum(grad, axis=0))
        d_second = norm_back(grad, normed_two, inverse_two, norm2_gain)
        g_down_bias = lax.optimization_barrier(jnp.sum(d_second, axis=0))
        d_second_half = d_second.astype(jnp.bfloat16)
        g_down = jnp.dot(act_half.T, d_second_half, preferred_element_type=jnp.float32)
        d_pre = jnp.dot(d_second_half, down_weight.T, preferred_element_type=jnp.float32) * slope
        g_up_bias = lax.optimization_barrier(jnp.sum(d_pre, axis=0))
        d_pre_half = d_pre.astype(jnp.bfloat16)
        g_up = jnp.dot(hidden_half.T, d_pre_half, preferred_element_type=jnp.float32)
        d_hidden = d_second + jnp.dot(d_pre_half, up_weight.T, preferred_element_type=jnp.float32)
        g_gain_one = lax.optimization_barrier(jnp.sum(d_hidden * normed_one, axis=0))
        g_bias_one = lax.optimization_barrier(jnp.sum(d_hidden, axis=0))
        d_first = norm_back(d_hidden, normed_one, inverse_one, norm1_gain)
        g_out_bias = lax.optimization_barrier(jnp.sum(d_first, axis=0))
        d_first_half = d_first.astype(jnp.bfloat16)
        g_out = jnp.dot(context.T, d_first_half, preferred_element_type=jnp.float32)
        d_context = jnp.dot(d_first_half, out_weight.T, preferred_element_type=jnp.float32).astype(jnp.bfloat16)
        d_queries, d_keys, d_values = attend_back(split_heads(queries), split_heads(keys), split_heads(values), segs, lse, split_heads(d_context))
        d_queries = d_queries.reshape(SEQ, D)
        d_keys = d_keys.reshape(SEQ, D)
        d_values = d_values.reshape(SEQ, D)
        g_qv_bias = jnp.stack([lax.optimization_barrier(jnp.sum(d_queries, axis=0)), lax.optimization_barrier(jnp.sum(d_values, axis=0))])
        halves = [d_queries.astype(jnp.bfloat16), d_keys.astype(jnp.bfloat16), d_values.astype(jnp.bfloat16)]
        g_qkv = jnp.stack([jnp.dot(rows.T, halves[slot], preferred_element_type=jnp.float32) for slot in range(3)])
        d_input = d_first
        for slot in range(3):
            d_input = d_input + jnp.dot(halves[slot], qkv_weight[slot].T, preferred_element_type=jnp.float32)
        terms = (g_qkv, g_qv_bias, g_out, g_out_bias, g_gain_one, g_bias_one, g_up, g_up_bias, g_down, g_down_bias, g_gain_two, g_bias_two)
        new_totals = tuple((total + term for total, term in zip(totals, terms)))
        return (new_totals, (output.astype(jnp.bfloat16), d_input.astype(jnp.bfloat16)))
    zero_init = (jnp.zeros((3, D, D), jnp.float32), jnp.zeros((2, D), jnp.float32), jnp.zeros((D, D), jnp.float32), jnp.zeros((D,), jnp.float32), jnp.zeros((D,), jnp.float32), jnp.zeros((D,), jnp.float32), jnp.zeros((D, FF), jnp.float32), jnp.zeros((FF,), jnp.float32), jnp.zeros((FF, D), jnp.float32), jnp.zeros((D,), jnp.float32), jnp.zeros((D,), jnp.float32), jnp.zeros((D,), jnp.float32))
    totals, (outputs, grads) = lax.scan(one_sequence, zero_init, (inputs, segment_ids, cots))
    return (outputs.reshape(TOKENS, D), grads.reshape(TOKENS, D), totals[0], totals[1], totals[2], totals[3], totals[4], totals[5], totals[6], totals[7], totals[8], totals[9], totals[10], totals[11])
```

```python
import jax
import jax.numpy as jnp
from jax import lax
from jax.experimental import pallas as pl
from jax.experimental.pallas import tpu as pltpu
from jax.sharding import PartitionSpec as P

HEAD_DIM = 64


EPS = 1e-12
MASKED = -1e30
ROOT_HALF = 0.7071067811865476
INV_ROOT_TAU = 0.3989422804014327


def layer_norm(rows, gain, shift):
    center = rows - jnp.mean(rows, axis=-1, keepdims=True)
    inverse = lax.rsqrt(jnp.mean(center * center, axis=-1, keepdims=True) + EPS)
    normed = center * inverse
    return (normed * gain + shift, normed, inverse)


def norm_back(grad, normed, inverse, gain):
    scaled = grad * gain
    return inverse * (
        scaled
        - jnp.mean(scaled, axis=-1, keepdims=True)
        - normed * jnp.mean(scaled * normed, axis=-1, keepdims=True)
    )


def gelu_parts(pre):
    cumul = 0.5 * (1.0 + lax.erf(pre * ROOT_HALF))
    return (pre * cumul, cumul + pre * jnp.exp(-0.5 * pre * pre) * INV_ROOT_TAU)


def masked_scores(queries, keys, segs):
    scores = jnp.einsum(
        "qhd,khd->hqk", queries, keys, preferred_element_type=jnp.float32
    ) * HEAD_DIM ** (-0.5)
    allowed = segs[:, None] == segs[None, :]
    return jnp.where(allowed[None], scores, MASKED)


def forward_seq(items):
    queries, keys, values, segs = items
    masked = masked_scores(queries, keys, segs)
    top = jnp.max(masked, axis=-1, keepdims=True)
    lse = top + jnp.log(jnp.sum(jnp.exp(masked - top), axis=-1, keepdims=True))
    probs = jnp.exp(masked - lse).astype(jnp.bfloat16)
    context = jnp.einsum("hqk,khd->qhd", probs, values, preferred_element_type=jnp.float32)
    return (context.astype(jnp.bfloat16), lse)


def backward_seq(items):
    queries, keys, values, segs, lse, d_context = items
    masked = masked_scores(queries, keys, segs)
    probs = jnp.exp(masked - lse)
    probs_half = probs.astype(jnp.bfloat16)
    d_values = jnp.einsum("hqk,qhd->khd", probs_half, d_context, preferred_element_type=jnp.float32)
    d_probs = jnp.einsum("qhd,khd->hqk", d_context, values, preferred_element_type=jnp.float32)
    d_scores = (
        probs * (d_probs - jnp.sum(probs * d_probs, axis=-1, keepdims=True)) * HEAD_DIM ** (-0.5)
    )
    d_scores = d_scores.astype(jnp.bfloat16)
    d_queries = jnp.einsum("hqk,khd->qhd", d_scores, keys, preferred_element_type=jnp.float32)
    d_keys = jnp.einsum("hqk,qhd->khd", d_scores, queries, preferred_element_type=jnp.float32)
    return (d_queries, d_keys, d_values)


def contract_rows(left, right):
    return lax.dot_general(
        left, right, (((0,), (0,)), ((), ())), preferred_element_type=jnp.float32
    )


def contract_cols(left, right):
    return lax.dot_general(
        left, right, (((1,), (1,)), ((), ())), preferred_element_type=jnp.float32
    )


MESH = pl.DeviceIdType.MESH


def places():
    dp, me = lax.axis_index("dp"), lax.axis_index("tensor")
    core, x, z = lax.rem(me, 2), lax.rem(me // 2, 4), me // 8
    right, left = lax.rem(x + 1, 4), lax.rem(x + 3, 4)

    def at(z_at, x_at, core_at):
        return z_at * 8 + x_at * 2 + core_at

    return dp, me, core, x, z, right, left, at


def meet(dp, partners):
    barrier = pltpu.get_barrier_semaphore()
    for partner in partners:
        pl.semaphore_signal(barrier, inc=1, device_id=(dp, partner), device_id_type=MESH)
    pl.semaphore_wait(barrier, len(partners))


def gather_kernel(x_ref, out_ref, send, recv, local):
    dp, me, core, x, z, right, left, at = places()
    far, other = 1 - z, 1 - core
    across = lax.rem(x + 2, 4)
    z_peer, c_peer = at(far, x, core), at(z, x, other)
    r_peer, l_peer = at(z, right, core), at(z, left, core)
    meet(dp, (z_peer, c_peer, r_peer, l_peer))
    started = []
    numbers = {}

    def copy(name, src, slot, half, peer):
        number = numbers.setdefault(name, len(numbers))
        return pltpu.make_async_remote_copy(
            src_ref=src,
            dst_ref=out_ref.at[slot, half],
            send_sem=send.at[number],
            recv_sem=recv.at[number],
            device_id=(dp, peer),
            device_id_type=MESH,
        )

    def push(name, src, slot, half, peer):
        moving = copy(name, src, slot, half, peer)
        moving.start()
        started.append(moving)

    def arrived(name, slot, half):
        copy(name, out_ref.at[slot, half], slot, half, me).wait_recv()

    def share(level, name_x, slot, half):
        push(("c", level, name_x, half), out_ref.at[slot, half], slot, half, c_peer)

    for half in range(2):
        push(("z", half), x_ref.at[half], me, half, z_peer)
    for step in range(2):
        push(("r", 0, step), x_ref.at[step], me, step, r_peer)
        push(("l", 0, 1 - step), x_ref.at[1 - step], me, 1 - step, l_peer)
    for half in range(2):
        push(("c", 0, "own", half), x_ref.at[half], me, half, c_peer)
    keep = pltpu.make_async_copy(x_ref, out_ref.at[me], local)
    keep.start()

    for level, z_at in ((0, z), (1, far)):
        if level == 1:
            own = at(far, x, core)
            for half in range(2):
                arrived(("z", half), own, half)
                push(("r", 1, half), out_ref.at[own, half], own, half, r_peer)
                push(("l", 1, half), out_ref.at[own, half], own, half, l_peer)
                share(1, "own", own, half)
        from_left, from_right = at(z_at, left, core), at(z_at, right, core)
        arrived(("r", level, 0), from_left, 0)
        push(("rr", level), out_ref.at[from_left, 0], from_left, 0, r_peer)
        share(level, "left", from_left, 0)
        arrived(("l", level, 1), from_right, 1)
        push(("ll", level), out_ref.at[from_right, 1], from_right, 1, l_peer)
        share(level, "right", from_right, 1)
        arrived(("r", level, 1), from_left, 1)
        share(level, "left", from_left, 1)
        arrived(("l", level, 0), from_right, 0)
        share(level, "right", from_right, 0)
    for level, z_at in ((0, z), (1, far)):
        beyond = at(z_at, across, core)
        arrived(("rr", level), beyond, 0)
        share(level, "across", beyond, 0)
        arrived(("ll", level), beyond, 1)
        share(level, "across", beyond, 1)
    for level, z_at in ((0, z), (1, far)):
        for name_x, x_at in (("own", x), ("left", left), ("right", right), ("across", across)):
            for half in range(2):
                arrived(("c", level, name_x, half), at(z_at, x_at, other), half)
    keep.wait()
    for moving in started:
        moving.wait_send()


def gather_tensor(block):
    rows, width = block.shape
    half = rows // 2
    out = pl.pallas_call(
        gather_kernel,
        out_shape=jax.ShapeDtypeStruct((16, 2, half, width), block.dtype),
        in_specs=[pl.BlockSpec(memory_space=pltpu.VMEM)],
        out_specs=pl.BlockSpec(memory_space=pltpu.VMEM),
        scratch_shapes=[
            pltpu.SemaphoreType.DMA((30,)),
            pltpu.SemaphoreType.DMA((30,)),
            pltpu.SemaphoreType.DMA,
        ],
        compiler_params=pltpu.CompilerParams(
            collective_id=0, has_side_effects=True, vmem_limit_bytes=32 << 20
        ),
        cost_estimate=pl.CostEstimate(flops=0, bytes_accessed=60 << 20, transcendentals=0),
    )(block.reshape(2, half, width))
    return out.reshape(16 * rows, width)


def scatter_kernel(p_ref, out_ref, from_core, ring, from_z, send, recv):
    dp, me, core, x, z, right, left, at = places()
    far, other = 1 - z, 1 - core
    across = lax.rem(x + 2, 4)
    z_peer, c_peer = at(far, x, core), at(z, x, other)
    r_peer, l_peer = at(z, right, core), at(z, left, core)
    meet(dp, (z_peer, c_peer, r_peer, l_peer))
    started = []
    numbers = {}
    rows = out_ref.shape[1]

    def copy(name, src, dst, peer):
        number = numbers.setdefault(name, len(numbers))
        return pltpu.make_async_remote_copy(
            src_ref=src,
            dst_ref=dst,
            send_sem=send.at[number],
            recv_sem=recv.at[number],
            device_id=(dp, peer),
            device_id_type=MESH,
        )

    def push(name, src, dst, peer):
        moving = copy(name, src, dst, peer)
        moving.start()
        started.append(moving)

    def arrived(name, dst):
        copy(name, dst, dst, me).wait_recv()

    def total(dst, *terms):
        @pl.loop(0, rows // 16)
        def _(step):
            here = pl.ds(pl.multiple_of(step * 16, 16), 16)
            value = terms[0][here, :].astype(jnp.float32)
            for term in terms[1:]:
                value = value + term[here, :].astype(jnp.float32)
            dst[here, :] = value.astype(dst.dtype)

    order = [(level, kind) for level in (0, 1) for kind in range(4)]
    z_of = (far, z)
    x_of = (across, right, left, x)
    for level, kind in order:
        slot = level * 4 + kind
        push(
            ("c", slot),
            p_ref.at[at(z_of[level], x_of[kind], other)],
            from_core.at[slot],
            c_peer,
        )
    for level in range(2):
        base = level * 6

        def mine(kind, half):
            return from_core.at[level * 4 + kind, half]

        for kind in range(4):
            slot = level * 4 + kind
            arrived(("c", slot), from_core.at[slot])
            block = at(z_of[level], x_of[kind], core)
            for half in range(2):
                total(mine(kind, half), p_ref.at[block, half], mine(kind, half))
            if kind == 0:
                push(("ar", level), mine(0, 0), ring.at[base], r_peer)
                push(("al", level), mine(0, 1), ring.at[base + 1], l_peer)
            if kind == 1:
                push(("b", level, 2), mine(1, 1), ring.at[base + 2], r_peer)
            if kind == 2:
                push(("b", level, 3), mine(2, 0), ring.at[base + 3], l_peer)
        arrived(("ar", level), ring.at[base])
        total(mine(1, 0), ring.at[base], mine(1, 0))
        push(("b", level, 4), mine(1, 0), ring.at[base + 4], r_peer)
        arrived(("al", level), ring.at[base + 1])
        total(mine(2, 1), ring.at[base + 1], mine(2, 1))
        push(("b", level, 5), mine(2, 1), ring.at[base + 5], l_peer)
    for level in range(2):
        base = level * 6
        own = level * 4 + 3
        for half, parts in ((1, (2, 5)), (0, (3, 4))):
            for part in parts:
                arrived(("b", level, part), ring.at[base + part])
            terms = [from_core.at[own, half]] + [ring.at[base + part] for part in parts]
            if level == 0:
                total(from_core.at[own, half], *terms)
                push(("z", half), from_core.at[own, half], from_z.at[half], z_peer)
            else:
                arrived(("z", half), from_z.at[half])
                total(out_ref.at[half], *terms, from_z.at[half])
    for moving in started:
        moving.wait_send()


def scatter_tensor(whole):
    tokens, width = whole.shape
    half = tokens // 32
    wide = whole.dtype == jnp.float32
    out = pl.pallas_call(
        scatter_kernel,
        out_shape=jax.ShapeDtypeStruct((2, half, width), jnp.float32),
        in_specs=[pl.BlockSpec(memory_space=pltpu.VMEM)],
        out_specs=pl.BlockSpec(memory_space=pltpu.VMEM),
        scratch_shapes=[
            pltpu.VMEM((8, 2, half, width), whole.dtype),
            pltpu.VMEM((12, half, width), whole.dtype),
            pltpu.VMEM((2, half, width), whole.dtype),
            pltpu.SemaphoreType.DMA((22,)),
            pltpu.SemaphoreType.DMA((22,)),
        ],
        compiler_params=pltpu.CompilerParams(
            collective_id=2 if wide else 1, has_side_effects=True, vmem_limit_bytes=40 << 20
        ),
        cost_estimate=pl.CostEstimate(flops=0, bytes_accessed=80 << 20, transcendentals=0),
    )(whole.reshape(16, 2, half, width))
    return out.reshape(2 * half, width)


def per_device(
    block_input,
    segment_ids,
    qkv_weight,
    qv_bias,
    out_weight,
    out_bias,
    norm1_gain,
    norm1_bias,
    up_weight,
    up_bias,
    down_weight,
    down_bias,
    norm2_gain,
    norm2_bias,
    cotangent,
):
    width = qkv_weight.shape[2]
    seq_count, seq_len = segment_ids.shape
    heads_here = width // HEAD_DIM
    gathered = gather_tensor(block_input)
    tokens = gathered.shape[0]
    projected = jnp.einsum("td,cdw->ctw", gathered, qkv_weight, preferred_element_type=jnp.float32)
    queries = (projected[0] + qv_bias[0]).astype(jnp.bfloat16)
    keys = projected[1].astype(jnp.bfloat16)
    values = (projected[2] + qv_bias[1]).astype(jnp.bfloat16)

    def per_sequence(arr):
        return arr.reshape(seq_count, seq_len, heads_here, HEAD_DIM)

    seq_queries = per_sequence(queries)
    seq_keys = per_sequence(keys)
    seq_values = per_sequence(values)
    context, lse = lax.map(forward_seq, (seq_queries, seq_keys, seq_values, segment_ids))
    context = context.reshape(tokens, width)
    piece = context
    attended = scatter_tensor(
        jnp.dot(piece, out_weight, preferred_element_type=jnp.float32).astype(jnp.bfloat16)
    )
    first = block_input.astype(jnp.float32) + attended + out_bias
    hidden, normed_one, inverse_one = layer_norm(first, norm1_gain, norm1_bias)
    hidden_half = gather_tensor(hidden.astype(jnp.bfloat16))
    pre = jnp.dot(hidden_half, up_weight, preferred_element_type=jnp.float32) + up_bias
    act, slope = gelu_parts(pre)
    act_half = act.astype(jnp.bfloat16)
    piece = act_half
    down_sum = scatter_tensor(
        jnp.dot(piece, down_weight, preferred_element_type=jnp.float32).astype(jnp.bfloat16)
    )
    second = hidden + down_sum + down_bias
    output, normed_two, inverse_two = layer_norm(second, norm2_gain, norm2_bias)
    grad = cotangent.astype(jnp.float32)
    g_gain_two = jnp.sum(grad * normed_two, axis=0)
    g_bias_two = jnp.sum(grad, axis=0)
    d_second = norm_back(grad, normed_two, inverse_two, norm2_gain)
    g_down_bias = jnp.sum(d_second, axis=0)
    d_second_all = gather_tensor(d_second.astype(jnp.bfloat16))
    g_down = contract_rows(act_half, d_second_all)
    d_pre = contract_cols(d_second_all, down_weight) * slope
    g_up_bias = jnp.sum(d_pre, axis=0)
    d_pre_half = d_pre.astype(jnp.bfloat16)
    g_up = contract_rows(hidden_half, d_pre_half)
    piece = d_pre_half
    d_hidden = d_second + scatter_tensor(contract_cols(piece, up_weight))
    g_gain_one = jnp.sum(d_hidden * normed_one, axis=0)
    g_bias_one = jnp.sum(d_hidden, axis=0)
    d_first = norm_back(d_hidden, normed_one, inverse_one, norm1_gain)
    g_out_bias = jnp.sum(d_first, axis=0)
    d_first_all = gather_tensor(d_first.astype(jnp.bfloat16))
    g_out = contract_rows(context, d_first_all)
    d_context = contract_cols(d_first_all, out_weight).astype(jnp.bfloat16)
    d_queries, d_keys, d_values = lax.map(
        backward_seq, (seq_queries, seq_keys, seq_values, segment_ids, lse, per_sequence(d_context))
    )
    d_queries = d_queries.reshape(tokens, width)
    d_keys = d_keys.reshape(tokens, width)
    d_values = d_values.reshape(tokens, width)
    g_qv_bias = jnp.stack([jnp.sum(d_queries, axis=0), jnp.sum(d_values, axis=0)])
    d_qkv = jnp.stack([d_queries, d_keys, d_values]).astype(jnp.bfloat16)
    g_qkv = jnp.einsum("td,ctw->cdw", gathered, d_qkv, preferred_element_type=jnp.float32)
    piece = d_qkv
    input_grad = (
        d_first
        + scatter_tensor(
            jnp.einsum("ctw,cdw->td", piece, qkv_weight, preferred_element_type=jnp.float32).astype(
                jnp.bfloat16
            )
        )
    ).astype(jnp.bfloat16)
    g_qkv, g_qv_bias, g_out, g_up, g_up_bias, g_down = (
        lax.psum(g_qkv.astype(jnp.bfloat16), "dp").astype(jnp.float32),
        lax.psum(g_qv_bias.astype(jnp.bfloat16), "dp").astype(jnp.float32),
        lax.psum(g_out.astype(jnp.bfloat16), "dp").astype(jnp.float32),
        lax.psum(g_up.astype(jnp.bfloat16), "dp").astype(jnp.float32),
        lax.psum(g_up_bias.astype(jnp.bfloat16), "dp").astype(jnp.float32),
        lax.psum(g_down.astype(jnp.bfloat16), "dp").astype(jnp.float32),
    )
    g_out_bias, g_gain_one, g_bias_one, g_down_bias, g_gain_two, g_bias_two = lax.psum(
        (g_out_bias, g_gain_one, g_bias_one, g_down_bias, g_gain_two, g_bias_two), ("dp", "tensor")
    )
    return (
        output.astype(jnp.bfloat16),
        input_grad,
        g_qkv,
        g_qv_bias,
        g_out,
        g_out_bias,
        g_gain_one,
        g_bias_one,
        g_up,
        g_up_bias,
        g_down,
        g_down_bias,
        g_gain_two,
        g_bias_two,
    )


def solution(mesh):
    placed = (
        P(("dp", "tensor"), None),
        P("dp", None),
        P(None, None, "tensor"),
        P(None, "tensor"),
        P("tensor", None),
        P(),
        P(),
        P(),
        P(None, "tensor"),
        P("tensor"),
        P("tensor", None),
        P(),
        P(),
        P(),
        P(("dp", "tensor"), None),
    )
    return jax.shard_map(
        per_device,
        mesh=mesh,
        in_specs=placed,
        out_specs=(
            P(("dp", "tensor"), None),
            P(("dp", "tensor"), None),
            P(None, None, "tensor"),
            P(None, "tensor"),
            P("tensor", None),
            P(),
            P(),
            P(),
            P(None, "tensor"),
            P("tensor"),
            P("tensor", None),
            P(),
            P(),
            P(),
        ),
        check_vma=False,
    )
```
